256 devices in a mesh: section: 16 (over y_hi, x, core), slab: 16 (over z, y_lo).
Axes of the slice: x: 4, y: 4 (y_hi: 2, y_lo: 2; y = y_hi * 2 + y_lo), z: 8, core: 2. Of those that a mesh axis runs over, the one named last changes fastest.
Arguments:
- fwd_states: bfloat16 [16, 128, 32, 512], P('section', None, 'slab'), may hold values from -6 to 6
- back_states: bfloat16 [16, 128, 32, 512], P('section', None, 'slab'), may hold values from -6 to 6
- back_grads: bfloat16 [16, 128, 32, 512], P('section', None, 'slab'), may hold values from -6 to 6
- batch_in: bfloat16 [128, 32, 512], P(None, 'slab'), may hold values from -6 to 6
- head_state: bfloat16 [128, 32, 512], P(None, 'slab'), may hold values from -6 to 6
- head_grad: bfloat16 [128, 32, 512], P(None, 'slab'), may hold values from -6 to 6
- couplings: bfloat16 [16, 4, 27, 64, 64], P('section'), may hold values from -0.15625 to 0.15625
Outputs:
- fwd_out: bfloat16 [16, 128, 32, 512], P('section', None, 'slab')
- back_in: bfloat16 [16, 128, 32, 512], P('section', None, 'slab')
- back_grad: bfloat16 [16, 128, 32, 512], P('section', None, 'slab')
The draws below stay inside these ranges and needn't reach their ends.
All inputs are finite; a program needn't handle non-finite values.
Results may differ from the reference program's by a relative error of at most 0.006.
Values may be sent and summed in bfloat16 or wider, within the bound.
A program may use at most 128 MiB of HBM per device.

```python
import jax
import jax.numpy as jnp
from jax import lax

HALF = 64
HGT = 16
WID = 32
PAIRS = 2
DEPTH = 32
SECTIONS = 16
N_SECTION = 16


def shard_levels(own_key, shape, cuts, low, top_value):
    factor_of, own = 1.0, jax.random.fold_in(own_key, 6)
    for dim, parts in cuts:
        heights = jnp.exp(jax.random.uniform(jax.random.fold_in(own, dim), (parts,), jnp.float32, low / len(cuts), top_value / len(cuts)))
        factor_of = factor_of * jnp.repeat(heights, shape[dim] // parts).reshape([-1 if axis == dim else 1 for axis in range(len(shape))])
    return factor_of


def noise(stream_key, shape, scale, reach, pieces=(), kind=jnp.bfloat16):
    factor_of = shard_levels(stream_key, shape, pieces, -0.22, 0.18) if pieces else 1.0
    values = jax.random.normal(stream_key, shape, jnp.float32) * scale * factor_of
    return jnp.minimum(jnp.maximum(values, -reach), reach).astype(kind)


def setup_inputs(seed: int = 0) -> dict:
    arg_keys = jax.random.split(jax.random.key(seed), 8)
    fwd_states = noise(arg_keys[0], (SECTIONS, 2 * HALF, DEPTH, HGT * WID), 1.0, 6.0, ((0, 16), (2, 16)))
    back_states = noise(arg_keys[1], (SECTIONS, 2 * HALF, DEPTH, HGT * WID), 1.0, 6.0, ((0, 16), (2, 16)))
    back_grads = noise(arg_keys[2], (SECTIONS, 2 * HALF, DEPTH, HGT * WID), 1.0, 6.0, ((0, 16), (2, 16)))
    batch_in = noise(arg_keys[3], (2 * HALF, DEPTH, HGT * WID), 1.0, 6.0, ((1, 16),))
    head_state = noise(arg_keys[4], (2 * HALF, DEPTH, HGT * WID), 1.0, 6.0, ((1, 16),))
    head_grad = noise(arg_keys[5], (2 * HALF, DEPTH, HGT * WID), 1.0, 6.0, ((1, 16),))
    couplings = noise(arg_keys[6], (SECTIONS, 2 * PAIRS, 27, HALF, HALF), (27 * HALF) ** -0.5, 0.15625, ((0, 16),))
    return {"fwd_states": fwd_states, "back_states": back_states, "back_grads": back_grads, "batch_in": batch_in, "head_state": head_state, "head_grad": head_grad, "couplings": couplings}


def conv_ref(field, kernels):
    chans = field.shape[0]
    outs = kernels.shape[1]
    lhs = field.astype(jnp.float32).reshape(1, chans, field.shape[1], HGT, WID)
    kern = kernels.astype(jnp.float32).reshape(3, 3, 3, outs, chans).transpose(3, 4, 0, 1, 2)
    result = lax.conv_general_dilated(lhs, kern, (1, 1, 1), ((1, 1), (1, 1), (1, 1)), dimension_numbers=("NCDHW", "OIDHW", "NCDHW"), precision=lax.Precision.HIGHEST)
    return result[0].reshape(outs, field.shape[1], HGT * WID)


def flipped(kernels):
    return jnp.swapaxes(jnp.flip(kernels, 0), 1, 2)


def slope(z):
    sig = jax.nn.sigmoid(z)
    return sig * (1.0 + z * (1.0 - sig))


def one_section(source, target, target_grad, kernels):
    state = source
    for pair in range(PAIRS):
        first, second = state[:HALF], state[HALF:]
        upper = (first.astype(jnp.float32) + jax.nn.silu(conv_ref(second, kernels[2 * pair]))).astype(jnp.bfloat16)
        lower = (second.astype(jnp.float32) + jax.nn.silu(conv_ref(upper, kernels[2 * pair + 1]))).astype(jnp.bfloat16)
        state = jnp.concatenate([upper, lower], 0)
    ystate = target
    grads = target_grad.astype(jnp.float32)
    for pair in range(PAIRS - 1, -1, -1):
        upper, lower = ystate[:HALF], ystate[HALF:]
        grad_up, grad_low = grads[:HALF], grads[HALF:]
        zeta_g = conv_ref(upper, kernels[2 * pair + 1])
        second = (lower.astype(jnp.float32) - jax.nn.silu(zeta_g)).astype(jnp.bfloat16)
        zeta_f = conv_ref(second, kernels[2 * pair])
        first = (upper.astype(jnp.float32) - jax.nn.silu(zeta_f)).astype(jnp.bfloat16)
        inner_u = (slope(zeta_g) * grad_low).astype(jnp.bfloat16)
        carry_up = grad_up + conv_ref(inner_u, flipped(kernels[2 * pair + 1]))
        inner_w = (slope(zeta_f) * carry_up).astype(jnp.bfloat16)
        carry_low = grad_low + conv_ref(inner_w, flipped(kernels[2 * pair]))
        ystate = jnp.concatenate([first, second], 0)
        grads = jnp.concatenate([carry_up, carry_low], 0)
    return state, ystate, grads.astype(jnp.bfloat16)


def reference(fwd_states, back_states, back_grads, batch_in, head_state, head_grad, couplings):
    def per_section(index):
        prior = fwd_states[jnp.maximum(index - 1, 0)]
        source = jnp.where(index == 0, batch_in, prior)
        later = jnp.minimum(index + 1, N_SECTION - 1)
        target = jnp.where(index == N_SECTION - 1, head_state, back_states[later])
        target_grad = jnp.where(index == N_SECTION - 1, head_grad, back_grads[later])
        return one_section(source, target, target_grad, couplings[index])

    return lax.map(per_section, jnp.arange(N_SECTION, dtype=jnp.int32))
```

```python
import functools

import jax
import jax.numpy as jnp
from jax import lax
from jax.experimental import pallas as pl
from jax.experimental.pallas import tpu as pltpu
from jax.sharding import PartitionSpec as P

WID = 32
CELLS = 512
HALF = 64
PAIR = 2 * HALF
PAIRS = 2
MESH = pl.DeviceIdType.MESH
BF16 = jnp.bfloat16
F32 = jnp.float32


def swapped(section, slab):
    return (2 * (section // 2) + slab % 2, 2 * (slab // 2) + section % 2)


def lanes(rows):
    return lax.broadcasted_iota(jnp.int32, (rows, CELLS), 1)


def conv_pair(field, weights):
    col = lanes(1) % WID
    left = pltpu.roll(field, 1, 1) * (col >= 1).astype(BF16)
    right = pltpu.roll(field, CELLS - 1, 1) * (col <= WID - 2).astype(BF16)
    operand = jnp.concatenate([left, field, right], 0)
    sums = jnp.dot(weights, operand, preferred_element_type=F32)
    lane = lanes(PAIR)
    above = jnp.where(lane >= WID, pltpu.roll(sums[:PAIR], WID, 1), 0.0)
    below = jnp.where(lane < CELLS - WID, pltpu.roll(sums[2 * PAIR :], CELLS - WID, 1), 0.0)
    return sums[PAIR : 2 * PAIR] + above + below


def silu_slope(z):
    sig = jax.nn.sigmoid(z)
    return z * sig, sig * (1.0 + z * (1.0 - sig))


def step_kernel(
    n_section, n_slab,
    fwd_ref, state_ref, grad_ref, batch_ref, head_ref, head_grad_ref, kern_ref,
    out_fwd, out_back, out_grad,
    raw, kern, toep, toep_t,
    y1w, y2w, g2w, x1w, x2w, b_x2, b_u, b_w, b_x1, c_x2, c_u, c_w, f_y1, f_y2, d_y1, h2, stage,
    init_send, init_recv, halo_send, halo_recv, out_send, out_recv, kern_sem,
):
    a, b = lax.axis_index("section"), lax.axis_index("slab")
    section, slab = swapped(a, b)
    home_here = a % 2 == b % 2
    has_lo, has_hi = slab > 0, slab < n_slab - 1
    lo_dev, hi_dev = swapped(section, slab - 1), swapped(section, slab + 1)
    up_dev = swapped((a + 1) % n_section, b)
    down_dev = swapped((a + n_section - 1) % n_section, b)

    kern_local = pltpu.make_async_copy(kern_ref, kern, kern_sem.at[0])
    kern_remote = pltpu.make_async_remote_copy(
        kern_ref, kern, kern_sem.at[1], kern_sem.at[2],
        device_id=(a + 1 - 2 * (a % 2), b), device_id_type=MESH,
    )
    pl.when(home_here)(kern_local.start)

    barrier = pltpu.get_barrier_semaphore()

    def greet(device):
        pl.semaphore_signal(barrier, inc=1, device_id=device, device_id_type=MESH)

    greet(((section + n_section - 1) % n_section, slab))
    greet(((section + 1) % n_section, slab))
    pl.when(has_lo)(lambda: greet(lo_dev))
    pl.when(has_hi)(lambda: greet(hi_dev))
    pl.when(jnp.logical_not(home_here))(lambda: greet((section, slab)))
    peers = [has_lo, has_hi, jnp.logical_not(home_here)]
    pl.semaphore_wait(barrier, 2 + sum(peer.astype(jnp.int32) for peer in peers))

    def init_copy(index, source, device):
        half = index % 2
        return pltpu.make_async_remote_copy(
            source.at[pl.ds(half * HALF, HALF)], raw.at[index], init_send.at[index], init_recv.at[index],
            device_id=device, device_id_type=MESH,
        )

    for index, usual, other, device, is_end in (
        (0, state_ref, head_ref, down_dev, a == 0),
        (1, state_ref, head_ref, down_dev, a == 0),
        (3, grad_ref, head_grad_ref, down_dev, a == 0),
        (2, grad_ref, head_grad_ref, down_dev, a == 0),
        (5, fwd_ref, batch_ref, up_dev, a == n_section - 1),
        (4, fwd_ref, batch_ref, up_dev, a == n_section - 1),
    ):
        pl.when(is_end)(init_copy(index, other, device).start)
        pl.when(jnp.logical_not(is_end))(init_copy(index, usual, device).start)

    pl.when(home_here)(kern_remote.start)

    row = lax.broadcasted_iota(jnp.int32, (PAIR, PAIR), 0)
    col = lax.broadcasted_iota(jnp.int32, (PAIR, PAIR), 1)
    split = (col == 2 * (row % HALF) + row // HALF).astype(BF16)
    eye = (row == col).astype(BF16)[:HALF, :HALF]

    for ref, width in ((y1w, 2), (y2w, 1), (g2w, 1), (x2w, 2), (x1w, 1), (b_w, 2), (b_x1, 2), (f_y2, 2), (c_w, 1)):
        rows = width * HALF
        zero = jnp.zeros((rows, CELLS), BF16)

        @pl.when(jnp.logical_not(has_lo))
        def _():
            ref[:rows] = zero

        @pl.when(jnp.logical_not(has_hi))
        def _():
            ref[rows + PAIR :] = zero

    pl.when(home_here)(kern_local.wait)
    pl.when(jnp.logical_not(home_here))(kern_remote.wait_recv)

    def band(step, carry):
        which, b_off = step // 3, step % 3
        blank = jnp.zeros((HALF, HALF), BF16)
        for c_off in range(3):
            taps = [kern[which, 9 * depth + 3 * b_off + c_off] for depth in range(3)]
            line = jnp.concatenate(taps, 1)
            back = [kern[which, 26 - (9 * depth + 3 * b_off + c_off)] for depth in range(3)]
            line_t = lax.dot_general(
                eye, jnp.concatenate(back, 0), (((1,), (1,)), ((), ())), preferred_element_type=F32
            ).astype(BF16)
            for plane in range(2):
                where = (which, pl.ds(pl.multiple_of(b_off * PAIR, PAIR) + plane * HALF, HALF), pl.ds(c_off * 256, 256))
                order = (lambda t: [t, blank]) if plane == 0 else (lambda t: [blank, t])
                toep[where] = jnp.concatenate(order(line), 1)
                toep_t[where] = jnp.concatenate(order(line_t), 1)
        return carry

    lax.fori_loop(0, 6 * PAIRS, band, 0)

    def halo(index, ref, width):
        rows = width * HALF

        def copy(side, source, target, device):
            return pltpu.make_async_remote_copy(
                ref.at[pl.ds(source, rows)], ref.at[pl.ds(target, rows)],
                halo_send.at[index, side], halo_recv.at[index, side],
                device_id=device, device_id_type=MESH,
            )

        low = copy(0, rows, rows + PAIR, lo_dev)
        high = copy(1, PAIR, 0, hi_dev)
        return low, high

    def halo_start(*spec):
        low, high = halo(*spec)
        pl.when(has_lo)(low.start)
        pl.when(has_hi)(high.start)

    def halo_wait(*spec):
        low, high = halo(*spec)
        pl.when(has_lo)(high.wait_recv)
        pl.when(has_hi)(low.wait_recv)

    def halo_done(*spec):
        low, high = halo(*spec)
        pl.when(has_lo)(low.wait_send)
        pl.when(has_hi)(high.wait_send)

    def arrived(index):
        init_copy(index, state_ref, down_dev).wait_recv()
        return jnp.dot(split, raw[index].reshape(PAIR, CELLS), preferred_element_type=F32)

    def out_copy(index, out, half):
        local = pltpu.make_async_copy(stage.at[index], out.at[half], out_send.at[index])
        remote = pltpu.make_async_remote_copy(
            stage.at[index], out.at[half], out_send.at[index], out_recv.at[index],
            device_id=(section, slab), device_id_type=MESH,
        )
        return local, remote

    outs = ((out_fwd, 0), (out_fwd, 1), (out_back, 0), (out_back, 1), (out_grad, 0), (out_grad, 1))

    def out_start(index, value):
        stage[index] = value
        local, remote = out_copy(index, *outs[index])
        pl.when(home_here)(local.start)
        pl.when(jnp.logical_not(home_here))(remote.start)

    edge_row = lax.broadcasted_iota(jnp.int32, (PAIR, CELLS), 0)
    outside = (
        jnp.logical_and(edge_row < HALF, jnp.logical_not(has_lo)),
        jnp.logical_and(edge_row >= HALF, jnp.logical_not(has_hi)),
    )

    def inside(side, value):
        return jnp.where(outside[side], 0.0, value).astype(BF16)

    halos = {
        "y1": (0, y1w, 2), "y2": (1, y2w, 1), "g2": (2, g2w, 1), "x2": (3, x2w, 2), "x1": (4, x1w, 1),
        "w": (5, b_w, 2), "bx1": (6, b_x1, 2), "fy2": (7, f_y2, 2), "cw": (8, c_w, 1),
    }

    y1w[PAIR : 2 * PAIR] = arrived(0).astype(BF16)
    halo_start(*halos["y1"])
    y2w[HALF : HALF + PAIR] = arrived(1).astype(BF16)
    halo_start(*halos["y2"])
    g2w[HALF : HALF + PAIR] = arrived(3).astype(BF16)
    halo_start(*halos["g2"])
    h1 = arrived(2)

    def backward_head(pair, upper, lower, lower_grad, second, inner):
        for side in range(2):
            rows = pl.ds(side * PAIR, PAIR)
            zeta = conv_pair(upper[pl.ds(side * PAIR, 4 * HALF)], toep[2 * pair + 1])
            silu, slope = silu_slope(zeta)
            second[rows] = inside(side, lower[rows].astype(F32) - silu)
            inner[rows] = inside(side, slope * lower_grad(side))

    def backward_tail(pair, upper, second, inner, grad_up):
        silu, slope = silu_slope(conv_pair(second[...], toep[2 * pair]))
        first = (upper[PAIR : 2 * PAIR].astype(F32) - silu).astype(BF16)
        grad_up = grad_up + conv_pair(inner[...], toep_t[2 * pair + 1])
        return first, grad_up, (slope * grad_up).astype(BF16)

    def forward(pair, upper, lower, mixed):
        for side in range(2):
            rows = pl.ds(side * PAIR, PAIR)
            zeta = conv_pair(lower[pl.ds(side * PAIR, 4 * HALF)], toep[2 * pair])
            mixed[rows] = inside(side, upper[rows].astype(F32) + silu_slope(zeta)[0])
        zeta = conv_pair(mixed[...], toep[2 * pair + 1])
        return (lower[PAIR : 2 * PAIR].astype(F32) + silu_slope(zeta)[0]).astype(BF16)

    for name in ("y1", "y2", "g2"):
        halo_wait(*halos[name])
    backward_head(1, y1w, y2w, lambda side: g2w[pl.ds(side * PAIR, PAIR)].astype(F32), b_x2, b_u)
    first, h1, inner_w = backward_tail(1, y1w, b_x2, b_u, h1)
    b_w[PAIR : 2 * PAIR] = inner_w
    halo_start(*halos["w"])
    b_x1[PAIR : 2 * PAIR] = first
    halo_start(*halos["bx1"])

    x2w[PAIR : 2 * PAIR] = arrived(5).astype(BF16)
    halo_start(*halos["x2"])
    x1w[HALF : HALF + PAIR] = arrived(4).astype(BF16)
    halo_start(*halos["x1"])
    halo_wait(*halos["x2"])
    halo_wait(*halos["x1"])
    f_y2[PAIR : 2 * PAIR] = forward(0, x1w, x2w, f_y1)
    halo_start(*halos["fy2"])

    halo_wait(*halos["w"])
    for side in range(2):
        rows = pl.ds(side * PAIR, PAIR)
        h2[rows] = g2w[rows].astype(F32) + conv_pair(b_w[pl.ds(side * PAIR, 4 * HALF)], toep_t[2])
    halo_wait(*halos["bx1"])
    backward_head(0, b_x1, b_x2, lambda side: h2[pl.ds(side * PAIR, PAIR)], c_x2, c_u)
    first, h1, inner_w = backward_tail(0, b_x1, c_x2, c_u, h1)
    c_w[HALF : HALF + PAIR] = inner_w
    halo_start(*halos["cw"])
    out_start(2, first)
    out_start(3, c_x2[HALF : HALF + PAIR])
    out_start(4, h1.astype(BF16))

    halo_wait(*halos["fy2"])
    lower = forward(1, f_y1, f_y2, d_y1)
    out_start(0, d_y1[HALF : HALF + PAIR])
    out_start(1, lower)

    halo_wait(*halos["cw"])
    out_start(5, (h2[HALF : HALF + PAIR] + conv_pair(c_w[...], toep_t[0])).astype(BF16))

    for index in range(6):
        init_copy(index, state_ref, down_dev).wait_send()
        local, remote = out_copy(index, *outs[index])
        pl.when(home_here)(local.wait)
        pl.when(jnp.logical_not(home_here))(remote.wait)
    pl.when(home_here)(kern_remote.wait_send)
    for spec in halos.values():
        halo_done(*spec)


def shards(fwd_states, back_states, back_grads, batch_in, head_state, head_grad, couplings):
    n_section, n_slab = lax.axis_size("section"), lax.axis_size("slab")
    anywhere = pl.BlockSpec(memory_space=pl.ANY)
    field = lambda planes: pltpu.VMEM((planes * HALF, CELLS), BF16)
    dma = pltpu.SemaphoreType.DMA
    out = jax.ShapeDtypeStruct((2, PAIR, CELLS), BF16)
    results = pl.pallas_call(
        functools.partial(step_kernel, n_section, n_slab),
        out_shape=(out, out, out),
        in_specs=[anywhere] * 7,
        out_specs=(anywhere,) * 3,
        scratch_shapes=[
            pltpu.VMEM((6, HALF, 2, CELLS), BF16),
            pltpu.VMEM(couplings.shape[1:], BF16),
            pltpu.VMEM((2 * PAIRS, 3 * PAIR, 12 * HALF), BF16),
            pltpu.VMEM((2 * PAIRS, 3 * PAIR, 12 * HALF), BF16),
            field(6), field(4), field(4), field(4), field(6),
            field(4), field(4), field(6), field(6),
            field(4), field(4), field(4),
            field(4), field(6), field(4),
            pltpu.VMEM((2 * PAIR, CELLS), F32),
            pltpu.VMEM((6, PAIR, CELLS), BF16),
            dma((6,)), dma((6,)), dma((9, 2)), dma((9, 2)), dma((6,)), dma((6,)), dma((3,)),
        ],
        compiler_params=pltpu.CompilerParams(collective_id=0, has_side_effects=True),
    )(fwd_states[0], back_states[0], back_grads[0], batch_in, head_state, head_grad, couplings[0])

    def placed(value):
        planes = value.reshape(2, 2, HALF, CELLS)
        return jnp.transpose(planes, (0, 2, 1, 3)).reshape(1, 2 * HALF, 2, CELLS)

    return tuple(placed(value) for value in results)


def solution(mesh):
    return jax.shard_map(
        shards,
        mesh=mesh,
        in_specs=(
            P("section", None, "slab", None),
            P("section", None, "slab", None),
            P("section", None, "slab", None),
            P(None, "slab", None),
            P(None, "slab", None),
            P(None, "slab", None),
            P("section", None, None, None, None),
        ),
        out_specs=(
            P("section", None, "slab", None),
            P("section", None, "slab", None),
            P("section", None, "slab", None),
        ),
        check_vma=False,
    )
```

```python
import functools

import jax
import jax.numpy as jnp
from jax import lax
from jax.experimental import pallas as pl
from jax.experimental.pallas import tpu as pltpu
from jax.sharding import PartitionSpec as P

WID = 32
CELLS = 512
HALF = 64
PAIR = 2 * HALF
PAIRS = 2
MESH = pl.DeviceIdType.MESH
BF16 = jnp.bfloat16
F32 = jnp.float32


def swapped(section, slab):
    return (2 * (section // 2) + slab % 2, 2 * (slab // 2) + section % 2)


def lanes(rows):
    return lax.broadcasted_iota(jnp.int32, (rows, CELLS), 1)


def conv_pair(field, weights):
    col = lanes(1) % WID
    left = pltpu.roll(field, 1, 1) * (col >= 1).astype(BF16)
    right = pltpu.roll(field, CELLS - 1, 1) * (col <= WID - 2).astype(BF16)
    operand = jnp.concatenate([left, field, right], 0)
    sums = jnp.dot(weights, operand, preferred_element_type=F32)
    lane = lanes(PAIR)
    above = jnp.where(lane >= WID, pltpu.roll(sums[:PAIR], WID, 1), 0.0)
    below = jnp.where(lane < CELLS - WID, pltpu.roll(sums[2 * PAIR :], CELLS - WID, 1), 0.0)
    return sums[PAIR : 2 * PAIR] + above + below


def silu_slope(z):
    sig = jax.nn.sigmoid(z)
    return z * sig, sig * (1.0 + z * (1.0 - sig))


def step_kernel(
    n_section, n_slab,
    fwd_ref, state_ref, grad_ref, batch_ref, head_ref, head_grad_ref, kern_ref,
    out_fwd, out_back, out_grad,
    raw, kern, toep, toep_t,
    y1w, y2w, g2w, x1w, x2w, b_x2, b_u, b_w, b_x1, c_x2, c_u, c_w, f_y1, f_y2, d_y1, h2, zeta, stage,
    init_send, init_recv, halo_send, halo_recv, out_send, out_recv, kern_sem,
):
    a, b = lax.axis_index("section"), lax.axis_index("slab")
    section, slab = swapped(a, b)
    home_here = a % 2 == b % 2
    has_lo, has_hi = slab > 0, slab < n_slab - 1
    lo_dev, hi_dev = swapped(section, slab - 1), swapped(section, slab + 1)
    up_dev, down_dev = swapped(a + 1, b), swapped(a - 1, b)

    kern_local = pltpu.make_async_copy(kern_ref, kern, kern_sem.at[0])
    kern_remote = pltpu.make_async_remote_copy(
        kern_ref, kern, kern_sem.at[1], kern_sem.at[2],
        device_id=(a + 1 - 2 * (a % 2), b), device_id_type=MESH,
    )
    pl.when(home_here)(kern_local.start)

    barrier = pltpu.get_barrier_semaphore()

    def greet(device):
        pl.semaphore_signal(barrier, inc=1, device_id=device, device_id_type=MESH)

    greet((jnp.where(section == 0, 1, section - 1), slab))
    greet((jnp.where(section == n_section - 1, n_section - 2, section + 1), slab))
    pl.when(has_lo)(lambda: greet(lo_dev))
    pl.when(has_hi)(lambda: greet(hi_dev))
    pl.when(jnp.logical_not(home_here))(lambda: greet((section, slab)))
    peers = [has_lo, has_hi, jnp.logical_not(home_here), a > 0, a < n_section - 1, a == 1, a == n_section - 2]
    pl.semaphore_wait(barrier, sum(peer.astype(jnp.int32) for peer in peers))

    def init_copy(index, source, device):
        half = index % 2
        return pltpu.make_async_remote_copy(
            source.at[pl.ds(half * HALF, HALF)], raw.at[index], init_send.at[index], init_recv.at[index],
            device_id=device, device_id_type=MESH,
        )

    def init_start(index, source, edge_source, device, edge_device, last, edge):
        pl.when(jnp.logical_not(last))(init_copy(index, source, device).start)
        pl.when(edge)(init_copy(index, edge_source, edge_device).start)

    def init_done(index, device, edge_device, last, edge):
        pl.when(jnp.logical_not(last))(init_copy(index, state_ref, device).wait_send)
        pl.when(edge)(init_copy(index, state_ref, edge_device).wait_send)

    down = (down_dev, swapped(n_section - 1, b), a == 0, a == n_section - 2)
    up = (up_dev, swapped(0, b), a == n_section - 1, a == 1)
    for index, source, edge_source in ((0, state_ref, head_ref), (1, state_ref, head_ref), (3, grad_ref, head_grad_ref)):
        init_start(index, source, edge_source, *down)

    def forward_start():
        for index in (5, 4):
            init_start(index, fwd_ref, batch_ref, *up)
    pl.when(home_here)(kern_remote.start)

    row = lax.broadcasted_iota(jnp.int32, (PAIR, PAIR), 0)
    col = lax.broadcasted_iota(jnp.int32, (PAIR, PAIR), 1)
    split = (col == 2 * (row % HALF) + row // HALF).astype(BF16)
    merge = (col == HALF * (row % 2) + row // 2).astype(BF16)
    eye = (row == col).astype(BF16)[:HALF, :HALF]

    for ref, width in ((y1w, 2), (y2w, 1), (g2w, 1), (x2w, 2), (x1w, 1), (b_w, 2), (b_x1, 2), (f_y2, 2), (c_w, 1)):
        rows = width * HALF
        zero = jnp.zeros((rows, CELLS), BF16)

        @pl.when(jnp.logical_not(has_lo))
        def _():
            ref[:rows] = zero

        @pl.when(jnp.logical_not(has_hi))
        def _():
            ref[rows + PAIR :] = zero

    pl.when(home_here)(kern_local.wait)
    pl.when(jnp.logical_not(home_here))(kern_remote.wait_recv)
    pl.when(jnp.logical_not(home_here))(forward_start)

    def band(step, carry):
        which, b_off = step // 3, step % 3
        blank = jnp.zeros((HALF, HALF), BF16)
        for c_off in range(3):
            taps = [kern[which, 9 * depth + 3 * b_off + c_off] for depth in range(3)]
            line = jnp.concatenate(taps, 1)
            back = [kern[which, 26 - (9 * depth + 3 * b_off + c_off)] for depth in range(3)]
            line_t = lax.dot_general(
                eye, jnp.concatenate(back, 0), (((1,), (1,)), ((), ())), preferred_element_type=F32
            ).astype(BF16)
            for plane in range(2):
                where = (which, pl.ds(pl.multiple_of(b_off * PAIR, PAIR) + plane * HALF, HALF), pl.ds(c_off * 256, 256))
                order = (lambda t: [t, blank]) if plane == 0 else (lambda t: [blank, t])
                toep[where] = jnp.concatenate(order(line), 1)
                toep_t[where] = jnp.concatenate(order(line_t), 1)
        return carry

    lax.fori_loop(0, 6 * PAIRS, band, 0)
    pl.when(home_here)(forward_start)

    def halo(index, ref, width):
        rows = width * HALF

        def copy(side, source, target, device):
            return pltpu.make_async_remote_copy(
                ref.at[pl.ds(source, rows)], ref.at[pl.ds(target, rows)],
                halo_send.at[index, side], halo_recv.at[index, side],
                device_id=device, device_id_type=MESH,
            )

        low = copy(0, rows, rows + PAIR, lo_dev)
        high = copy(1, PAIR, 0, hi_dev)
        return low, high

    def halo_start(*spec):
        low, high = halo(*spec)
        pl.when(has_lo)(low.start)
        pl.when(has_hi)(high.start)

    def halo_wait(*spec):
        low, high = halo(*spec)
        pl.when(has_lo)(high.wait_recv)
        pl.when(has_hi)(low.wait_recv)

    def halo_done(*spec):
        low, high = halo(*spec)
        pl.when(has_lo)(low.wait_send)
        pl.when(has_hi)(high.wait_send)

    def arrived(index):
        init_copy(index, state_ref, down_dev).wait_recv()
        return jnp.dot(split, raw[index].reshape(PAIR, CELLS), preferred_element_type=F32)

    def out_copy(index, out, half):
        local = pltpu.make_async_copy(stage.at[index], out.at[pl.ds(half * HALF, HALF)], out_send.at[index])
        remote = pltpu.make_async_remote_copy(
            stage.at[index], out.at[pl.ds(half * HALF, HALF)], out_send.at[index], out_recv.at[index],
            device_id=(section, slab), device_id_type=MESH,
        )
        return local, remote

    outs = ((out_fwd, 0), (out_fwd, 1), (out_back, 0), (out_back, 1), (out_grad, 0), (out_grad, 1))

    def out_start(index, value):
        rows = jnp.dot(merge, value, preferred_element_type=F32).astype(BF16)
        stage[index] = rows.reshape(HALF, 2, CELLS)
        local, remote = out_copy(index, *outs[index])
        pl.when(home_here)(local.start)
        pl.when(jnp.logical_not(home_here))(remote.start)

    edge_row = lax.broadcasted_iota(jnp.int32, (PAIR, CELLS), 0)
    outside = (
        jnp.logical_and(edge_row < HALF, jnp.logical_not(has_lo)),
        jnp.logical_and(edge_row >= HALF, jnp.logical_not(has_hi)),
    )

    def inside(side, value):
        return jnp.where(outside[side], 0.0, value).astype(BF16)

    halos = {
        "y1": (0, y1w, 2), "y2": (1, y2w, 1), "g2": (2, g2w, 1), "x2": (3, x2w, 2), "x1": (4, x1w, 1),
        "w": (5, b_w, 2), "bx1": (6, b_x1, 2), "fy2": (7, f_y2, 2), "cw": (8, c_w, 1),
    }

    y1w[PAIR : 2 * PAIR] = arrived(0).astype(BF16)
    halo_start(*halos["y1"])
    y2w[HALF : HALF + PAIR] = arrived(1).astype(BF16)
    halo_start(*halos["y2"])
    init_start(2, grad_ref, head_grad_ref, *down)
    g2w[HALF : HALF + PAIR] = arrived(3).astype(BF16)
    halo_start(*halos["g2"])
    x2w[PAIR : 2 * PAIR] = arrived(5).astype(BF16)
    halo_start(*halos["x2"])

    sides = [(side, pl.ds(side * PAIR, PAIR), pl.ds(side * PAIR, 4 * HALF)) for side in range(2)]

    def zeta_upper(pair, upper):
        for side, rows, wide in sides:
            zeta[rows] = conv_pair(upper[wide], toep[2 * pair + 1])

    def undo_second(lower, second):
        for side, rows, wide in sides:
            second[rows] = inside(side, lower[rows].astype(F32) - silu_slope(zeta[rows])[0])

    def undo_first(pair, upper, second):
        silu, slope = silu_slope(conv_pair(second[...], toep[2 * pair]))
        return (upper[PAIR : 2 * PAIR].astype(F32) - silu).astype(BF16), slope

    def grad_inner(lower_grad, inner):
        for side, rows, wide in sides:
            inner[rows] = inside(side, silu_slope(zeta[rows])[1] * lower_grad[rows].astype(F32))

    def forward(pair, upper, lower, mixed):
        for side, rows, wide in sides:
            z = conv_pair(lower[wide], toep[2 * pair])
            mixed[rows] = inside(side, upper[rows].astype(F32) + silu_slope(z)[0])
        z = conv_pair(mixed[...], toep[2 * pair + 1])
        return (lower[PAIR : 2 * PAIR].astype(F32) + silu_slope(z)[0]).astype(BF16)

    halo_wait(*halos["y1"])
    zeta_upper(1, y1w)
    x1w[HALF : HALF + PAIR] = arrived(4).astype(BF16)
    halo_start(*halos["x1"])
    halo_wait(*halos["y2"])
    undo_second(y2w, b_x2)
    first, slope = undo_first(1, y1w, b_x2)
    b_x1[PAIR : 2 * PAIR] = first
    halo_start(*halos["bx1"])
    halo_wait(*halos["g2"])
    grad_inner(g2w, b_u)
    h1 = conv_pair(b_u[...], toep_t[3]) + arrived(2)
    b_w[PAIR : 2 * PAIR] = (slope * h1).astype(BF16)
    halo_start(*halos["w"])

    halo_wait(*halos["x2"])
    halo_wait(*halos["x1"])
    f_y2[PAIR : 2 * PAIR] = forward(0, x1w, x2w, f_y1)
    halo_start(*halos["fy2"])

    halo_wait(*halos["bx1"])
    zeta_upper(0, b_x1)
    undo_second(b_x2, c_x2)
    out_start(3, c_x2[HALF : HALF + PAIR])
    first, slope = undo_first(0, b_x1, c_x2)
    out_start(2, first)
    halo_wait(*halos["w"])
    for side, rows, wide in sides:
        h2[rows] = g2w[rows].astype(F32) + conv_pair(b_w[wide], toep_t[2])
    grad_inner(h2, c_u)
    h1 = h1 + conv_pair(c_u[...], toep_t[1])
    c_w[HALF : HALF + PAIR] = (slope * h1).astype(BF16)
    halo_start(*halos["cw"])
    out_start(4, h1.astype(BF16))

    halo_wait(*halos["fy2"])
    lower = forward(1, f_y1, f_y2, d_y1)
    out_start(0, d_y1[HALF : HALF + PAIR])
    out_start(1, lower)

    halo_wait(*halos["cw"])
    out_start(5, (h2[HALF : HALF + PAIR] + conv_pair(c_w[...], toep_t[0])).astype(BF16))

    for index in range(6):
        init_done(index, *(down if index < 4 else up))
        local, remote = out_copy(index, *outs[index])
        pl.when(home_here)(local.wait)
        pl.when(jnp.logical_not(home_here))(remote.wait)
    pl.when(home_here)(kern_remote.wait_send)
    for spec in halos.values():
        halo_done(*spec)


def settle_kernel(in_0, in_1, in_2, out_0, out_1, out_2, buffer, sems):
    reads = [pltpu.make_async_copy(ref, buffer.at[i], sems.at[0, i]) for i, ref in enumerate((in_0, in_1, in_2))]
    writes = [pltpu.make_async_copy(buffer.at[i], ref, sems.at[1, i]) for i, ref in enumerate((out_0, out_1, out_2))]
    for copy in reads:
        copy.start()
    for read, write in zip(reads, writes):
        read.wait()
        write.start()
    for copy in writes:
        copy.wait()


def shards(fwd_states, back_states, back_grads, batch_in, head_state, head_grad, couplings):
    n_section, n_slab = lax.axis_size("section"), lax.axis_size("slab")
    anywhere = pl.BlockSpec(memory_space=pl.ANY)
    field = lambda planes: pltpu.VMEM((planes * HALF, CELLS), BF16)
    dma = pltpu.SemaphoreType.DMA
    out = jax.ShapeDtypeStruct((PAIR, 2, CELLS), BF16)
    results = pl.pallas_call(
        functools.partial(step_kernel, n_section, n_slab),
        out_shape=(out, out, out),
        in_specs=[anywhere] * 7,
        out_specs=(anywhere,) * 3,
        scratch_shapes=[
            pltpu.VMEM((6, HALF, 2, CELLS), BF16),
            pltpu.VMEM(couplings.shape[1:], BF16),
            pltpu.VMEM((2 * PAIRS, 3 * PAIR, 12 * HALF), BF16),
            pltpu.VMEM((2 * PAIRS, 3 * PAIR, 12 * HALF), BF16),
            field(6), field(4), field(4), field(4), field(6),
            field(4), field(4), field(6), field(6),
            field(4), field(4), field(4),
            field(4), field(6), field(4),
            pltpu.VMEM((2 * PAIR, CELLS), F32),
            pltpu.VMEM((2 * PAIR, CELLS), F32),
            pltpu.VMEM((6, HALF, 2, CELLS), BF16),
            dma((6,)), dma((6,)), dma((9, 2)), dma((9, 2)), dma((6,)), dma((6,)), dma((3,)),
        ],
        compiler_params=pltpu.CompilerParams(collective_id=0, has_side_effects=True),
    )(fwd_states[0], back_states[0], back_grads[0], batch_in, head_state, head_grad, couplings[0])

    settled = pl.pallas_call(
        settle_kernel,
        out_shape=(out, out, out),
        in_specs=[anywhere] * 3,
        out_specs=(anywhere,) * 3,
        scratch_shapes=[pltpu.VMEM((3, PAIR, 2, CELLS), BF16), dma((2, 3))],
    )(*results)
    return tuple(value[None] for value in settled)


def solution(mesh):
    return jax.shard_map(
        shards,
        mesh=mesh,
        in_specs=(
            P("section", None, "slab", None),
            P("section", None, "slab", None),
            P("section", None, "slab", None),
            P(None, "slab", None),
            P(None, "slab", None),
            P(None, "slab", None),
            P("section", None, None, None, None),
        ),
        out_specs=(
            P("section", None, "slab", None),
            P("section", None, "slab", None),
            P("section", None, "slab", None),
        ),
        check_vma=False,
    )
```

```python
import functools

import jax
import jax.numpy as jnp
from jax import lax
from jax.experimental import pallas as pl
from jax.experimental.pallas import tpu as pltpu
from jax.sharding import PartitionSpec as P

WID = 32
CELLS = 512
HALF = 64
PAIR = 2 * HALF
PAIRS = 2
RELAYED = (1, 2, 3)
MESH = pl.DeviceIdType.MESH
BF16 = jnp.bfloat16
F32 = jnp.float32


def swapped(section, slab):
    return (2 * (section // 2) + slab % 2, 2 * (slab // 2) + section % 2)


def lanes(rows):
    return lax.broadcasted_iota(jnp.int32, (rows, CELLS), 1)


def conv_pair(field, weights):
    col = lanes(1) % WID
    left = pltpu.roll(field, 1, 1) * (col >= 1).astype(BF16)
    right = pltpu.roll(field, CELLS - 1, 1) * (col <= WID - 2).astype(BF16)
    operand = jnp.concatenate([left, field, right], 0)
    sums = jnp.dot(weights, operand, preferred_element_type=F32)
    lane = lanes(PAIR)
    above = jnp.where(lane >= WID, pltpu.roll(sums[:PAIR], WID, 1), 0.0)
    below = jnp.where(lane < CELLS - WID, pltpu.roll(sums[2 * PAIR :], CELLS - WID, 1), 0.0)
    return sums[PAIR : 2 * PAIR] + above + below


def silu_slope(z):
    sig = jax.nn.sigmoid(z)
    return z * sig, sig * (1.0 + z * (1.0 - sig))


def step_kernel(
    n_section, n_slab,
    fwd_ref, state_ref, grad_ref, batch_ref, head_ref, head_grad_ref, kern_ref,
    out_fwd, out_back, out_grad,
    raw, relay, kern, toep, toep_t,
    y1w, y2w, g2w, x1w, x2w, b_x2, b_u, b_w, b_x1, c_x2, c_u, c_w, f_y1, f_y2, d_y1, h2, zeta, stage,
    init_send, init_recv, relay_send, relay_recv, halo_send, halo_recv, out_send, out_recv, kern_sem,
):
    a, b = lax.axis_index("section"), lax.axis_index("slab")
    section, slab = swapped(a, b)
    home_here = a % 2 == b % 2
    has_lo, has_hi = slab > 0, slab < n_slab - 1
    lo_dev, hi_dev = swapped(section, slab - 1), swapped(section, slab + 1)
    up_dev, down_dev = swapped(a + 1, b), swapped(a - 1, b)

    kern_local = pltpu.make_async_copy(kern_ref, kern, kern_sem.at[0])
    kern_remote = pltpu.make_async_remote_copy(
        kern_ref, kern, kern_sem.at[1], kern_sem.at[2],
        device_id=(a + 1 - 2 * (a % 2), b), device_id_type=MESH,
    )
    pl.when(home_here)(kern_local.start)

    mid = n_section // 2
    odd_slab = b % 2 == 1
    sends_relayed = jnp.logical_and(a == mid, odd_slab)
    relays = jnp.logical_and(a == mid - 1, jnp.logical_not(odd_slab))
    gets_relayed = jnp.logical_and(a == mid - 1, odd_slab)

    barrier = pltpu.get_barrier_semaphore()

    def greet(device):
        pl.semaphore_signal(barrier, inc=1, device_id=device, device_id_type=MESH)

    greet((jnp.where(section == 0, 1, section - 1), slab))
    greet((jnp.where(section == n_section - 1, n_section - 2, section + 1), slab))
    pl.when(relays)(lambda: greet((a + 1, b + 1)))
    pl.when(gets_relayed)(lambda: greet((a, b - 1)))
    pl.when(has_lo)(lambda: greet(lo_dev))
    pl.when(has_hi)(lambda: greet(hi_dev))
    pl.when(jnp.logical_not(home_here))(lambda: greet((section, slab)))
    peers = [has_lo, has_hi, jnp.logical_not(home_here), a > 0, a < n_section - 1, a == 1, a == n_section - 2]
    peers += [sends_relayed, relays]
    pl.semaphore_wait(barrier, sum(peer.astype(jnp.int32) for peer in peers))

    def init_copy(index, source, device):
        half = index % 2
        return pltpu.make_async_remote_copy(
            source.at[pl.ds(half * HALF, HALF)], raw.at[index], init_send.at[index], init_recv.at[index],
            device_id=device, device_id_type=MESH,
        )

    def relay_in(index, source):
        half = index % 2
        return pltpu.make_async_remote_copy(
            source.at[pl.ds(half * HALF, HALF)], relay.at[index], init_send.at[index], relay_recv.at[index],
            device_id=(a - 1, b - 1), device_id_type=MESH,
        )

    def relay_out(index):
        return pltpu.make_async_remote_copy(
            relay.at[index], raw.at[index], relay_send.at[index], init_recv.at[index],
            device_id=(a, b + 1), device_id_type=MESH,
        )

    def relay_on(index):
        @pl.when(relays)
        def _():
            relay_in(index, state_ref).wait_recv()
            relay_out(index).start()

    def init_start(index, source, edge_source, device, edge_device, last, edge):
        if index in RELAYED:
            last = jnp.logical_or(last, sends_relayed)
            pl.when(sends_relayed)(relay_in(index, source).start)
        pl.when(jnp.logical_not(last))(init_copy(index, source, device).start)
        pl.when(edge)(init_copy(index, edge_source, edge_device).start)

    def init_done(index, device, edge_device, last, edge):
        pl.when(jnp.logical_not(last))(init_copy(index, state_ref, device).wait_send)
        pl.when(edge)(init_copy(index, state_ref, edge_device).wait_send)

    down = (down_dev, swapped(n_section - 1, b), a == 0, a == n_section - 2)
    up = (up_dev, swapped(0, b), a == n_section - 1, a == 1)
    for index, source, edge_source in ((0, state_ref, head_ref), (1, state_ref, head_ref), (3, grad_ref, head_grad_ref)):
        init_start(index, source, edge_source, *down)

    def forward_start():
        for index in (5, 4):
            init_start(index, fwd_ref, batch_ref, *up)
    pl.when(home_here)(kern_remote.start)

    row = lax.broadcasted_iota(jnp.int32, (PAIR, PAIR), 0)
    col = lax.broadcasted_iota(jnp.int32, (PAIR, PAIR), 1)
    split = (col == 2 * (row % HALF) + row // HALF).astype(BF16)
    merge = (col == HALF * (row % 2) + row // 2).astype(BF16)
    eye = (row == col).astype(BF16)[:HALF, :HALF]

    for ref, width in ((y1w, 2), (y2w, 1), (g2w, 1), (x2w, 2), (x1w, 1), (b_w, 2), (b_x1, 2), (f_y2, 2), (c_w, 1)):
        rows = width * HALF
        zero = jnp.zeros((rows, CELLS), BF16)

        @pl.when(jnp.logical_not(has_lo))
        def _():
            ref[:rows] = zero

        @pl.when(jnp.logical_not(has_hi))
        def _():
            ref[rows + PAIR :] = zero

    pl.when(home_here)(kern_local.wait)
    pl.when(jnp.logical_not(home_here))(kern_remote.wait_recv)
    pl.when(jnp.logical_not(home_here))(forward_start)

    def band(step, carry):
        which, b_off = step // 3, step % 3
        blank = jnp.zeros((HALF, HALF), BF16)
        for c_off in range(3):
            taps = [kern[which, 9 * depth + 3 * b_off + c_off] for depth in range(3)]
            line = jnp.concatenate(taps, 1)
            back = [kern[which, 26 - (9 * depth + 3 * b_off + c_off)] for depth in range(3)]
            line_t = lax.dot_general(
                eye, jnp.concatenate(back, 0), (((1,), (1,)), ((), ())), preferred_element_type=F32
            ).astype(BF16)
            for plane in range(2):
                where = (which, pl.ds(pl.multiple_of(b_off * PAIR, PAIR) + plane * HALF, HALF), pl.ds(c_off * 256, 256))
                order = (lambda t: [t, blank]) if plane == 0 else (lambda t: [blank, t])
                toep[where] = jnp.concatenate(order(line), 1)
                toep_t[where] = jnp.concatenate(order(line_t), 1)
        return carry

    lax.fori_loop(0, 6 * PAIRS, band, 0)
    pl.when(home_here)(forward_start)

    def halo(index, ref, width):
        rows = width * HALF

        def copy(side, source, target, device):
            return pltpu.make_async_remote_copy(
                ref.at[pl.ds(source, rows)], ref.at[pl.ds(target, rows)],
                halo_send.at[index, side], halo_recv.at[index, side],
                device_id=device, device_id_type=MESH,
            )

        low = copy(0, rows, rows + PAIR, lo_dev)
        high = copy(1, PAIR, 0, hi_dev)
        return low, high

    def halo_start(*spec):
        low, high = halo(*spec)
        pl.when(has_lo)(low.start)
        pl.when(has_hi)(high.start)

    def halo_wait(*spec):
        low, high = halo(*spec)
        pl.when(has_lo)(high.wait_recv)
        pl.when(has_hi)(low.wait_recv)

    def halo_done(*spec):
        low, high = halo(*spec)
        pl.when(has_lo)(low.wait_send)
        pl.when(has_hi)(high.wait_send)

    def arrived(index):
        init_copy(index, state_ref, down_dev).wait_recv()
        return jnp.dot(split, raw[index].reshape(PAIR, CELLS), preferred_element_type=F32)

    def out_copy(index, out, half):
        local = pltpu.make_async_copy(stage.at[index], out.at[pl.ds(half * HALF, HALF)], out_send.at[index])
        remote = pltpu.make_async_remote_copy(
            stage.at[index], out.at[pl.ds(half * HALF, HALF)], out_send.at[index], out_recv.at[index],
            device_id=(section, slab), device_id_type=MESH,
        )
        return local, remote

    outs = ((out_fwd, 0), (out_fwd, 1), (out_back, 0), (out_back, 1), (out_grad, 0), (out_grad, 1))

    def out_start(index, value):
        rows = jnp.dot(merge, value, preferred_element_type=F32).astype(BF16)
        stage[index] = rows.reshape(HALF, 2, CELLS)
        local, remote = out_copy(index, *outs[index])
        pl.when(home_here)(local.start)
        pl.when(jnp.logical_not(home_here))(remote.start)

    edge_row = lax.broadcasted_iota(jnp.int32, (PAIR, CELLS), 0)
    outside = (
        jnp.logical_and(edge_row < HALF, jnp.logical_not(has_lo)),
        jnp.logical_and(edge_row >= HALF, jnp.logical_not(has_hi)),
    )

    def inside(side, value):
        return jnp.where(outside[side], 0.0, value).astype(BF16)

    halos = {
        "y1": (0, y1w, 2), "y2": (1, y2w, 1), "g2": (2, g2w, 1), "x2": (3, x2w, 2), "x1": (4, x1w, 1),
        "w": (5, b_w, 2), "bx1": (6, b_x1, 2), "fy2": (7, f_y2, 2), "cw": (8, c_w, 1),
    }

    y1w[PAIR : 2 * PAIR] = arrived(0).astype(BF16)
    halo_start(*halos["y1"])
    y2w[HALF : HALF + PAIR] = arrived(1).astype(BF16)
    halo_start(*halos["y2"])
    relay_on(1)
    init_start(2, grad_ref, head_grad_ref, *down)
    g2w[HALF : HALF + PAIR] = arrived(3).astype(BF16)
    halo_start(*halos["g2"])
    relay_on(3)
    x2w[PAIR : 2 * PAIR] = arrived(5).astype(BF16)
    halo_start(*halos["x2"])

    sides = [(side, pl.ds(side * PAIR, PAIR), pl.ds(side * PAIR, 4 * HALF)) for side in range(2)]

    def zeta_upper(pair, upper):
        for side, rows, wide in sides:
            zeta[rows] = conv_pair(upper[wide], toep[2 * pair + 1])

    def undo_second(lower, second):
        for side, rows, wide in sides:
            second[rows] = inside(side, lower[rows].astype(F32) - silu_slope(zeta[rows])[0])

    def undo_first(pair, upper, second):
        silu, slope = silu_slope(conv_pair(second[...], toep[2 * pair]))
        return (upper[PAIR : 2 * PAIR].astype(F32) - silu).astype(BF16), slope

    def grad_inner(lower_grad, inner):
        for side, rows, wide in sides:
            inner[rows] = inside(side, silu_slope(zeta[rows])[1] * lower_grad[rows].astype(F32))

    def forward(pair, upper, lower, mixed, ready=lambda: None):
        for side, rows, wide in sides:
            z = conv_pair(lower[wide], toep[2 * pair])
            mixed[rows] = inside(side, upper[rows].astype(F32) + silu_slope(z)[0])
        ready()
        z = conv_pair(mixed[...], toep[2 * pair + 1])
        return (lower[PAIR : 2 * PAIR].astype(F32) + silu_slope(z)[0]).astype(BF16)

    halo_wait(*halos["y1"])
    zeta_upper(1, y1w)
    x1w[HALF : HALF + PAIR] = arrived(4).astype(BF16)
    halo_start(*halos["x1"])
    halo_wait(*halos["y2"])
    undo_second(y2w, b_x2)
    first, slope = undo_first(1, y1w, b_x2)
    b_x1[PAIR : 2 * PAIR] = first
    halo_start(*halos["bx1"])
    relay_on(2)
    halo_wait(*halos["g2"])
    grad_inner(g2w, b_u)
    h1 = conv_pair(b_u[...], toep_t[3]) + arrived(2)
    b_w[PAIR : 2 * PAIR] = (slope * h1).astype(BF16)
    halo_start(*halos["w"])

    halo_wait(*halos["x2"])
    halo_wait(*halos["x1"])
    f_y2[PAIR : 2 * PAIR] = forward(0, x1w, x2w, f_y1)
    halo_start(*halos["fy2"])

    halo_wait(*halos["bx1"])
    zeta_upper(0, b_x1)
    undo_second(b_x2, c_x2)
    out_start(3, c_x2[HALF : HALF + PAIR])
    first, slope = undo_first(0, b_x1, c_x2)
    out_start(2, first)
    halo_wait(*halos["w"])
    for side, rows, wide in sides:
        h2[rows] = g2w[rows].astype(F32) + conv_pair(b_w[wide], toep_t[2])
    grad_inner(h2, c_u)
    h1 = h1 + conv_pair(c_u[...], toep_t[1])
    c_w[HALF : HALF + PAIR] = (slope * h1).astype(BF16)
    halo_start(*halos["cw"])
    out_start(4, h1.astype(BF16))

    halo_wait(*halos["fy2"])
    out_start(1, forward(1, f_y1, f_y2, d_y1, lambda: out_start(0, d_y1[HALF : HALF + PAIR])))

    halo_wait(*halos["cw"])
    out_start(5, (h2[HALF : HALF + PAIR] + conv_pair(c_w[...], toep_t[0])).astype(BF16))

    for index in range(6):
        init_done(index, *(down if index < 4 else up))
        if index in RELAYED:
            pl.when(relays)(relay_out(index).wait_send)
        local, remote = out_copy(index, *outs[index])
        pl.when(home_here)(local.wait)
        pl.when(jnp.logical_not(home_here))(remote.wait)
    pl.when(home_here)(kern_remote.wait_send)
    for spec in halos.values():
        halo_done(*spec)


def settle_kernel(in_0, in_1, in_2, out_0, out_1, out_2, buffer, sems):
    reads = [pltpu.make_async_copy(ref, buffer.at[i], sems.at[0, i]) for i, ref in enumerate((in_0, in_1, in_2))]
    writes = [pltpu.make_async_copy(buffer.at[i], ref, sems.at[1, i]) for i, ref in enumerate((out_0, out_1, out_2))]
    for copy in reads:
        copy.start()
    for read, write in zip(reads, writes):
        read.wait()
        write.start()
    for copy in writes:
        copy.wait()


def shards(fwd_states, back_states, back_grads, batch_in, head_state, head_grad, couplings):
    n_section, n_slab = lax.axis_size("section"), lax.axis_size("slab")
    anywhere = pl.BlockSpec(memory_space=pl.ANY)
    field = lambda planes: pltpu.VMEM((planes * HALF, CELLS), BF16)
    dma = pltpu.SemaphoreType.DMA
    out = jax.ShapeDtypeStruct((PAIR, 2, CELLS), BF16)
    results = pl.pallas_call(
        functools.partial(step_kernel, n_section, n_slab),
        out_shape=(out, out, out),
        in_specs=[anywhere] * 7,
        out_specs=(anywhere,) * 3,
        scratch_shapes=[
            pltpu.VMEM((6, HALF, 2, CELLS), BF16),
            pltpu.VMEM((4, HALF, 2, CELLS), BF16),
            pltpu.VMEM(couplings.shape[1:], BF16),
            pltpu.VMEM((2 * PAIRS, 3 * PAIR, 12 * HALF), BF16),
            pltpu.VMEM((2 * PAIRS, 3 * PAIR, 12 * HALF), BF16),
            field(6), field(4), field(4), field(4), field(6),
            field(4), field(4), field(6), field(6),
            field(4), field(4), field(4),
            field(4), field(6), field(4),
            pltpu.VMEM((2 * PAIR, CELLS), F32),
            pltpu.VMEM((2 * PAIR, CELLS), F32),
            pltpu.VMEM((6, HALF, 2, CELLS), BF16),
            dma((6,)), dma((6,)), dma((4,)), dma((4,)), dma((9, 2)), dma((9, 2)), dma((6,)), dma((6,)), dma((3,)),
        ],
        compiler_params=pltpu.CompilerParams(collective_id=0, has_side_effects=True),
    )(fwd_states[0], back_states[0], back_grads[0], batch_in, head_state, head_grad, couplings[0])

    settled = pl.pallas_call(
        settle_kernel,
        out_shape=(out, out, out),
        in_specs=[anywhere] * 3,
        out_specs=(anywhere,) * 3,
        scratch_shapes=[pltpu.VMEM((3, PAIR, 2, CELLS), BF16), dma((2, 3))],
    )(*results)
    return tuple(value[None] for value in settled)


def solution(mesh):
    return jax.shard_map(
        shards,
        mesh=mesh,
        in_specs=(
            P("section", None, "slab", None),
            P("section", None, "slab", None),
            P("section", None, "slab", None),
            P(None, "slab", None),
            P(None, "slab", None),
            P(None, "slab", None),
            P("section", None, None, None, None),
        ),
        out_specs=(
            P("section", None, "slab", None),
            P("section", None, "slab", None),
            P("section", None, "slab", None),
        ),
        check_vma=False,
    )
```

```python
import functools

import jax
import jax.numpy as jnp
from jax import lax
from jax.experimental import pallas as pl
from jax.experimental.pallas import tpu as pltpu
from jax.sharding import PartitionSpec as P

WID = 32
CELLS = 512
HALF = 64
PAIR = 2 * HALF
PAIRS = 2
RELAYED = (1, 2, 3)
MESH = pl.DeviceIdType.MESH
BF16 = jnp.bfloat16
F32 = jnp.float32


def swapped(section, slab):
    return (2 * (section // 2) + slab % 2, 2 * (slab // 2) + section % 2)


def lanes(rows):
    return lax.broadcasted_iota(jnp.int32, (rows, CELLS), 1)


def conv_pair(field, weights):
    col = lanes(1) % WID
    left = pltpu.roll(field, 1, 1) * (col >= 1).astype(BF16)
    right = pltpu.roll(field, CELLS - 1, 1) * (col <= WID - 2).astype(BF16)
    operand = jnp.concatenate([left, field, right], 0)
    sums = jnp.dot(weights, operand, preferred_element_type=F32)
    lane = lanes(PAIR)
    above = jnp.where(lane >= WID, pltpu.roll(sums[:PAIR], WID, 1), 0.0)
    below = jnp.where(lane < CELLS - WID, pltpu.roll(sums[2 * PAIR :], CELLS - WID, 1), 0.0)
    return sums[PAIR : 2 * PAIR] + above + below


def silu_slope(z):
    sig = jax.nn.sigmoid(z)
    return z * sig, sig * (1.0 + z * (1.0 - sig))


def step_kernel(
    n_section, n_slab,
    fwd_ref, state_ref, grad_ref, batch_ref, head_ref, head_grad_ref, kern_ref,
    out_fwd, out_back, out_grad,
    raw, relay, kern, toep, toep_t,
    y1w, y2w, g2w, x1w, x2w, b_x2, b_u, b_w, b_x1, c_x2, c_u, c_w, f_y1, f_y2, d_y1, h2, zeta, stage,
    init_send, init_recv, relay_send, relay_recv, halo_send, halo_recv, out_send, out_recv, kern_sem,
):
    a, b = lax.axis_index("section"), lax.axis_index("slab")
    section, slab = swapped(a, b)
    home_here = a % 2 == b % 2
    has_lo, has_hi = slab > 0, slab < n_slab - 1
    lo_dev, hi_dev = swapped(section, slab - 1), swapped(section, slab + 1)
    up_dev, down_dev = swapped(a + 1, b), swapped(a - 1, b)

    kern_local = pltpu.make_async_copy(kern_ref, kern, kern_sem.at[0])
    kern_remote = pltpu.make_async_remote_copy(
        kern_ref, kern, kern_sem.at[1], kern_sem.at[2],
        device_id=(a + 1 - 2 * (a % 2), b), device_id_type=MESH,
    )
    pl.when(home_here)(kern_local.start)

    mid = n_section // 2
    odd_slab = b % 2 == 1
    sends_relayed = jnp.logical_and(a == mid, odd_slab)
    relays = jnp.logical_and(a == mid - 1, jnp.logical_not(odd_slab))
    gets_relayed = jnp.logical_and(a == mid - 1, odd_slab)

    barrier = pltpu.get_barrier_semaphore()

    def greet(device):
        pl.semaphore_signal(barrier, inc=1, device_id=device, device_id_type=MESH)

    greet((jnp.where(section == 0, 1, section - 1), slab))
    greet((jnp.where(section == n_section - 1, n_section - 2, section + 1), slab))
    pl.when(relays)(lambda: greet((a + 1, b + 1)))
    pl.when(gets_relayed)(lambda: greet((a, b - 1)))
    pl.when(has_lo)(lambda: greet(lo_dev))
    pl.when(has_hi)(lambda: greet(hi_dev))
    pl.when(jnp.logical_not(home_here))(lambda: greet((section, slab)))
    peers = [has_lo, has_hi, jnp.logical_not(home_here), a > 0, a < n_section - 1, a == 1, a == n_section - 2]
    peers += [sends_relayed, relays]
    pl.semaphore_wait(barrier, sum(peer.astype(jnp.int32) for peer in peers))

    def init_copy(index, source, device):
        half = index % 2
        return pltpu.make_async_remote_copy(
            source.at[pl.ds(half * HALF, HALF)], raw.at[index], init_send.at[index], init_recv.at[index],
            device_id=device, device_id_type=MESH,
        )

    def relay_in(index, source):
        half = index % 2
        return pltpu.make_async_remote_copy(
            source.at[pl.ds(half * HALF, HALF)], relay.at[index], init_send.at[index], relay_recv.at[index],
            device_id=(a - 1, b - 1), device_id_type=MESH,
        )

    def relay_out(index):
        return pltpu.make_async_remote_copy(
            relay.at[index], raw.at[index], relay_send.at[index], init_recv.at[index],
            device_id=(a, b + 1), device_id_type=MESH,
        )

    def relay_on(index):
        @pl.when(relays)
        def _():
            relay_in(index, state_ref).wait_recv()
            relay_out(index).start()

    def init_start(index, source, edge_source, device, edge_device, last, edge):
        if index in RELAYED:
            last = jnp.logical_or(last, sends_relayed)
            pl.when(sends_relayed)(relay_in(index, source).start)
        pl.when(jnp.logical_not(last))(init_copy(index, source, device).start)
        pl.when(edge)(init_copy(index, edge_source, edge_device).start)

    def init_done(index, device, edge_device, last, edge):
        pl.when(jnp.logical_not(last))(init_copy(index, state_ref, device).wait_send)
        pl.when(edge)(init_copy(index, state_ref, edge_device).wait_send)

    down = (down_dev, swapped(n_section - 1, b), a == 0, a == n_section - 2)
    up = (up_dev, swapped(0, b), a == n_section - 1, a == 1)
    for index, source, edge_source in ((0, state_ref, head_ref), (1, state_ref, head_ref), (3, grad_ref, head_grad_ref)):
        init_start(index, source, edge_source, *down)

    def forward_start(halves=(5, 4)):
        for index in halves:
            init_start(index, fwd_ref, batch_ref, *up)
    pl.when(home_here)(kern_remote.start)

    row = lax.broadcasted_iota(jnp.int32, (PAIR, PAIR), 0)
    col = lax.broadcasted_iota(jnp.int32, (PAIR, PAIR), 1)
    split = (col == 2 * (row % HALF) + row // HALF).astype(BF16)
    merge = (col == HALF * (row % 2) + row // 2).astype(BF16)
    eye = (row == col).astype(BF16)[:HALF, :HALF]

    for ref, width in ((y1w, 2), (y2w, 1), (g2w, 1), (x2w, 2), (x1w, 1), (b_w, 2), (b_x1, 2), (f_y2, 2), (c_w, 1)):
        rows = width * HALF
        zero = jnp.zeros((rows, CELLS), BF16)

        @pl.when(jnp.logical_not(has_lo))
        def _():
            ref[:rows] = zero

        @pl.when(jnp.logical_not(has_hi))
        def _():
            ref[rows + PAIR :] = zero

    pl.when(home_here)(kern_local.wait)
    pl.when(jnp.logical_not(home_here))(kern_remote.wait_recv)
    pl.when(jnp.logical_not(jnp.logical_or(home_here, relays)))(forward_start)
    pl.when(relays)(lambda: forward_start((5,)))

    def band(step, carry):
        which, b_off = step // 3, step % 3
        blank = jnp.zeros((HALF, HALF), BF16)
        for c_off in range(3):
            taps = [kern[which, 9 * depth + 3 * b_off + c_off] for depth in range(3)]
            line = jnp.concatenate(taps, 1)
            back = [kern[which, 26 - (9 * depth + 3 * b_off + c_off)] for depth in range(3)]
            line_t = lax.dot_general(
                eye, jnp.concatenate(back, 0), (((1,), (1,)), ((), ())), preferred_element_type=F32
            ).astype(BF16)
            for plane in range(2):
                where = (which, pl.ds(pl.multiple_of(b_off * PAIR, PAIR) + plane * HALF, HALF), pl.ds(c_off * 256, 256))
                order = (lambda t: [t, blank]) if plane == 0 else (lambda t: [blank, t])
                toep[where] = jnp.concatenate(order(line), 1)
                toep_t[where] = jnp.concatenate(order(line_t), 1)
        return carry

    lax.fori_loop(0, 6 * PAIRS, band, 0)
    pl.when(home_here)(forward_start)

    def halo(index, ref, width):
        rows = width * HALF

        def copy(side, source, target, device):
            return pltpu.make_async_remote_copy(
                ref.at[pl.ds(source, rows)], ref.at[pl.ds(target, rows)],
                halo_send.at[index, side], halo_recv.at[index, side],
                device_id=device, device_id_type=MESH,
            )

        low = copy(0, rows, rows + PAIR, lo_dev)
        high = copy(1, PAIR, 0, hi_dev)
        return low, high

    def halo_start(*spec):
        low, high = halo(*spec)
        pl.when(has_lo)(low.start)
        pl.when(has_hi)(high.start)

    def halo_wait(*spec):
        low, high = halo(*spec)
        pl.when(has_lo)(high.wait_recv)
        pl.when(has_hi)(low.wait_recv)

    def halo_done(*spec):
        low, high = halo(*spec)
        pl.when(has_lo)(low.wait_send)
        pl.when(has_hi)(high.wait_send)

    def arrived(index):
        init_copy(index, state_ref, down_dev).wait_recv()
        return jnp.dot(split, raw[index].reshape(PAIR, CELLS), preferred_element_type=F32)

    def out_copy(index, out, half):
        local = pltpu.make_async_copy(stage.at[index], out.at[pl.ds(half * HALF, HALF)], out_send.at[index])
        remote = pltpu.make_async_remote_copy(
            stage.at[index], out.at[pl.ds(half * HALF, HALF)], out_send.at[index], out_recv.at[index],
            device_id=(section, slab), device_id_type=MESH,
        )
        return local, remote

    outs = ((out_fwd, 0), (out_fwd, 1), (out_back, 0), (out_back, 1), (out_grad, 0), (out_grad, 1))

    def out_start(index, value):
        rows = jnp.dot(merge, value, preferred_element_type=F32).astype(BF16)
        stage[index] = rows.reshape(HALF, 2, CELLS)
        local, remote = out_copy(index, *outs[index])
        pl.when(home_here)(local.start)
        pl.when(jnp.logical_not(home_here))(remote.start)

    edge_row = lax.broadcasted_iota(jnp.int32, (PAIR, CELLS), 0)
    outside = (
        jnp.logical_and(edge_row < HALF, jnp.logical_not(has_lo)),
        jnp.logical_and(edge_row >= HALF, jnp.logical_not(has_hi)),
    )

    def inside(side, value):
        return jnp.where(outside[side], 0.0, value).astype(BF16)

    halos = {
        "y1": (0, y1w, 2), "y2": (1, y2w, 1), "g2": (2, g2w, 1), "x2": (3, x2w, 2), "x1": (4, x1w, 1),
        "w": (5, b_w, 2), "bx1": (6, b_x1, 2), "fy2": (7, f_y2, 2), "cw": (8, c_w, 1),
    }

    y1w[PAIR : 2 * PAIR] = arrived(0).astype(BF16)
    halo_start(*halos["y1"])
    relay_on(1)
    pl.when(relays)(lambda: forward_start((4,)))
    y2w[HALF : HALF + PAIR] = arrived(1).astype(BF16)
    halo_start(*halos["y2"])
    relay_on(3)
    init_start(2, grad_ref, head_grad_ref, *down)
    g2w[HALF : HALF + PAIR] = arrived(3).astype(BF16)
    halo_start(*halos["g2"])
    x2w[PAIR : 2 * PAIR] = arrived(5).astype(BF16)
    halo_start(*halos["x2"])

    sides = [(side, pl.ds(side * PAIR, PAIR), pl.ds(side * PAIR, 4 * HALF)) for side in range(2)]

    def zeta_upper(pair, upper):
        for side, rows, wide in sides:
            zeta[rows] = conv_pair(upper[wide], toep[2 * pair + 1])

    def undo_second(lower, second):
        for side, rows, wide in sides:
            second[rows] = inside(side, lower[rows].astype(F32) - silu_slope(zeta[rows])[0])

    def undo_first(pair, upper, second):
        silu, slope = silu_slope(conv_pair(second[...], toep[2 * pair]))
        return (upper[PAIR : 2 * PAIR].astype(F32) - silu).astype(BF16), slope

    def grad_inner(lower_grad, inner):
        for side, rows, wide in sides:
            inner[rows] = inside(side, silu_slope(zeta[rows])[1] * lower_grad[rows].astype(F32))

    def forward(pair, upper, lower, mixed, ready=lambda: None):
        for side, rows, wide in sides:
            z = conv_pair(lower[wide], toep[2 * pair])
            mixed[rows] = inside(side, upper[rows].astype(F32) + silu_slope(z)[0])
        ready()
        z = conv_pair(mixed[...], toep[2 * pair + 1])
        return (lower[PAIR : 2 * PAIR].astype(F32) + silu_slope(z)[0]).astype(BF16)

    halo_wait(*halos["y1"])
    zeta_upper(1, y1w)
    x1w[HALF : HALF + PAIR] = arrived(4).astype(BF16)
    halo_start(*halos["x1"])
    halo_wait(*halos["y2"])
    undo_second(y2w, b_x2)
    first, slope = undo_first(1, y1w, b_x2)
    b_x1[PAIR : 2 * PAIR] = first
    halo_start(*halos["bx1"])
    relay_on(2)
    halo_wait(*halos["g2"])
    grad_inner(g2w, b_u)
    h1 = conv_pair(b_u[...], toep_t[3]) + arrived(2)
    b_w[PAIR : 2 * PAIR] = (slope * h1).astype(BF16)
    halo_start(*halos["w"])

    halo_wait(*halos["x2"])
    halo_wait(*halos["x1"])
    f_y2[PAIR : 2 * PAIR] = forward(0, x1w, x2w, f_y1)
    halo_start(*halos["fy2"])

    halo_wait(*halos["bx1"])
    zeta_upper(0, b_x1)
    undo_second(b_x2, c_x2)
    out_start(3, c_x2[HALF : HALF + PAIR])
    first, slope = undo_first(0, b_x1, c_x2)
    out_start(2, first)
    halo_wait(*halos["w"])
    for side, rows, wide in sides:
        h2[rows] = g2w[rows].astype(F32) + conv_pair(b_w[wide], toep_t[2])
    grad_inner(h2, c_u)
    h1 = h1 + conv_pair(c_u[...], toep_t[1])
    c_w[HALF : HALF + PAIR] = (slope * h1).astype(BF16)
    halo_start(*halos["cw"])
    out_start(4, h1.astype(BF16))

    halo_wait(*halos["fy2"])
    out_start(1, forward(1, f_y1, f_y2, d_y1, lambda: out_start(0, d_y1[HALF : HALF + PAIR])))

    halo_wait(*halos["cw"])
    out_start(5, (h2[HALF : HALF + PAIR] + conv_pair(c_w[...], toep_t[0])).astype(BF16))

    for index in range(6):
        init_done(index, *(down if index < 4 else up))
        if index in RELAYED:
            pl.when(relays)(relay_out(index).wait_send)
        local, remote = out_copy(index, *outs[index])
        pl.when(home_here)(local.wait)
        pl.when(jnp.logical_not(home_here))(remote.wait)
    pl.when(home_here)(kern_remote.wait_send)
    for spec in halos.values():
        halo_done(*spec)


def settle_kernel(in_0, in_1, in_2, out_0, out_1, out_2, sems):
    copies = [
        pltpu.make_async_copy(source, target, sems.at[i])
        for i, (source, target) in enumerate(((in_0, out_0), (in_1, out_1), (in_2, out_2)))
    ]
    for copy in copies:
        copy.start()
    for copy in copies:
        copy.wait()


def shards(fwd_states, back_states, back_grads, batch_in, head_state, head_grad, couplings):
    n_section, n_slab = lax.axis_size("section"), lax.axis_size("slab")
    anywhere = pl.BlockSpec(memory_space=pl.ANY)
    field = lambda planes: pltpu.VMEM((planes * HALF, CELLS), BF16)
    dma = pltpu.SemaphoreType.DMA
    out = jax.ShapeDtypeStruct((PAIR, 2, CELLS), BF16)
    fields = (fwd_states[0], back_states[0], back_grads[0], batch_in, head_state, head_grad, couplings[0])
    results = pl.pallas_call(
        functools.partial(step_kernel, n_section, n_slab),
        out_shape=(out, out, out),
        in_specs=[pl.BlockSpec(memory_space=pltpu.HBM)] * 7,
        out_specs=(anywhere,) * 3,
        scratch_shapes=[
            pltpu.VMEM((6, HALF, 2, CELLS), BF16),
            pltpu.VMEM((4, HALF, 2, CELLS), BF16),
            pltpu.VMEM(couplings.shape[1:], BF16),
            pltpu.VMEM((2 * PAIRS, 3 * PAIR, 12 * HALF), BF16),
            pltpu.VMEM((2 * PAIRS, 3 * PAIR, 12 * HALF), BF16),
            field(6), field(4), field(4), field(4), field(6),
            field(4), field(4), field(6), field(6),
            field(4), field(4), field(4),
            field(4), field(6), field(4),
            pltpu.VMEM((2 * PAIR, CELLS), F32),
            pltpu.VMEM((2 * PAIR, CELLS), F32),
            pltpu.VMEM((6, HALF, 2, CELLS), BF16),
            dma((6,)), dma((6,)), dma((4,)), dma((4,)), dma((9, 2)), dma((9, 2)), dma((6,)), dma((6,)), dma((3,)),
        ],
        compiler_params=pltpu.CompilerParams(collective_id=0, has_side_effects=True, vmem_limit_bytes=32 << 20),
    )(*(pltpu.with_memory_space_constraint(field, pltpu.HBM) for field in fields))

    settled = pl.pallas_call(
        settle_kernel,
        out_shape=(out, out, out),
        in_specs=[anywhere] * 3,
        out_specs=(pl.BlockSpec(memory_space=pltpu.HBM),) * 3,
        scratch_shapes=[dma((3,))],
        compiler_params=pltpu.CompilerParams(vmem_limit_bytes=4 << 20),
    )(*results)
    return tuple(value[None] for value in settled)


def solution(mesh):
    return jax.shard_map(
        shards,
        mesh=mesh,
        in_specs=(
            P("section", None, "slab", None),
            P("section", None, "slab", None),
            P("section", None, "slab", None),
            P(None, "slab", None),
            P(None, "slab", None),
            P(None, "slab", None),
            P("section", None, None, None, None),
        ),
        out_specs=(
            P("section", None, "slab", None),
            P("section", None, "slab", None),
            P("section", None, "slab", None),
        ),
        check_vma=False,
    )
```

```python
import functools

import jax
import jax.numpy as jnp
from jax import lax
from jax.experimental import pallas as pl
from jax.experimental.pallas import tpu as pltpu
from jax.sharding import PartitionSpec as P

WID = 32
CELLS = 512
HALF = 64
PAIR = 2 * HALF
PAIRS = 2
RELAYED = (1, 2, 3)
MESH = pl.DeviceIdType.MESH
BF16 = jnp.bfloat16
F32 = jnp.float32


def swapped(section, slab):
    return (2 * (section // 2) + slab % 2, 2 * (slab // 2) + section % 2)


def lanes(rows):
    return lax.broadcasted_iota(jnp.int32, (rows, CELLS), 1)


def conv_pair(field, weights):
    col = lanes(1) % WID
    left = pltpu.roll(field, 1, 1) * (col >= 1).astype(BF16)
    right = pltpu.roll(field, CELLS - 1, 1) * (col <= WID - 2).astype(BF16)
    operand = jnp.concatenate([left, field, right], 0)
    sums = jnp.dot(weights, operand, preferred_element_type=F32)
    lane = lanes(PAIR)
    above = jnp.where(lane >= WID, pltpu.roll(sums[:PAIR], WID, 1), 0.0)
    below = jnp.where(lane < CELLS - WID, pltpu.roll(sums[2 * PAIR :], CELLS - WID, 1), 0.0)
    return sums[PAIR : 2 * PAIR] + above + below


def silu_slope(z):
    sig = jax.nn.sigmoid(z)
    return z * sig, sig * (1.0 + z * (1.0 - sig))


def step_kernel(
    n_section, n_slab,
    fwd_ref, state_ref, grad_ref, batch_ref, head_ref, head_grad_ref, kern_ref,
    out_fwd, out_back, out_grad,
    raw, relay, kern, toep, toep_t,
    y1w, y2w, g2w, x1w, x2w, b_x2, b_u, b_w, b_x1, c_x2, c_u, c_w, f_y1, f_y2, d_y1, h2, zeta, stage,
    init_send, init_recv, relay_send, relay_recv, halo_send, halo_recv, out_send, out_recv, kern_sem,
):
    a, b = lax.axis_index("section"), lax.axis_index("slab")
    section, slab = swapped(a, b)
    home_here = a % 2 == b % 2
    has_lo, has_hi = slab > 0, slab < n_slab - 1
    lo_dev, hi_dev = swapped(section, slab - 1), swapped(section, slab + 1)
    up_dev, down_dev = swapped(a + 1, b), swapped(a - 1, b)

    kern_local = pltpu.make_async_copy(kern_ref, kern, kern_sem.at[0])
    kern_remote = pltpu.make_async_remote_copy(
        kern_ref, kern, kern_sem.at[1], kern_sem.at[2],
        device_id=(a + 1 - 2 * (a % 2), b), device_id_type=MESH,
    )
    pl.when(home_here)(kern_local.start)

    mid = n_section // 2
    odd_slab = b % 2 == 1
    sends_relayed = jnp.logical_and(a == mid, odd_slab)
    relays = jnp.logical_and(a == mid - 1, jnp.logical_not(odd_slab))
    gets_relayed = jnp.logical_and(a == mid - 1, odd_slab)

    barrier = pltpu.get_barrier_semaphore()

    def greet(device):
        pl.semaphore_signal(barrier, inc=1, device_id=device, device_id_type=MESH)

    greet((jnp.where(section == 0, 1, section - 1), slab))
    greet((jnp.where(section == n_section - 1, n_section - 2, section + 1), slab))
    pl.when(relays)(lambda: greet((a + 1, b + 1)))
    pl.when(gets_relayed)(lambda: greet((a, b - 1)))
    pl.when(has_lo)(lambda: greet(lo_dev))
    pl.when(has_hi)(lambda: greet(hi_dev))
    pl.when(jnp.logical_not(home_here))(lambda: greet((section, slab)))
    peers = [has_lo, has_hi, jnp.logical_not(home_here), a > 0, a < n_section - 1, a == 1, a == n_section - 2]
    peers += [sends_relayed, relays]
    pl.semaphore_wait(barrier, sum(peer.astype(jnp.int32) for peer in peers))

    def init_copy(index, source, device):
        half = index % 2
        return pltpu.make_async_remote_copy(
            source.at[pl.ds(half * HALF, HALF)], raw.at[index], init_send.at[index], init_recv.at[index],
            device_id=device, device_id_type=MESH,
        )

    def relay_in(index, source):
        half = index % 2
        return pltpu.make_async_remote_copy(
            source.at[pl.ds(half * HALF, HALF)], relay.at[index], init_send.at[index], relay_recv.at[index],
            device_id=(a - 1, b - 1), device_id_type=MESH,
        )

    def relay_out(index):
        return pltpu.make_async_remote_copy(
            relay.at[index], raw.at[index], relay_send.at[index], init_recv.at[index],
            device_id=(a, b + 1), device_id_type=MESH,
        )

    def relay_on(index):
        @pl.when(relays)
        def _():
            relay_in(index, state_ref).wait_recv()
            relay_out(index).start()

    def init_start(index, source, edge_source, device, edge_device, last, edge):
        if index in RELAYED:
            last = jnp.logical_or(last, sends_relayed)
            pl.when(sends_relayed)(relay_in(index, source).start)
        pl.when(jnp.logical_not(last))(init_copy(index, source, device).start)
        pl.when(edge)(init_copy(index, edge_source, edge_device).start)

    def init_done(index, device, edge_device, last, edge):
        pl.when(jnp.logical_not(last))(init_copy(index, state_ref, device).wait_send)
        pl.when(edge)(init_copy(index, state_ref, edge_device).wait_send)

    down = (down_dev, swapped(n_section - 1, b), a == 0, a == n_section - 2)
    up = (up_dev, swapped(0, b), a == n_section - 1, a == 1)
    for index, source, edge_source in ((0, state_ref, head_ref), (1, state_ref, head_ref), (3, grad_ref, head_grad_ref)):
        init_start(index, source, edge_source, *down)

    def forward_start():
        for index in (5, 4):
            init_start(index, fwd_ref, batch_ref, *up)
    pl.when(home_here)(kern_remote.start)

    row = lax.broadcasted_iota(jnp.int32, (PAIR, PAIR), 0)
    col = lax.broadcasted_iota(jnp.int32, (PAIR, PAIR), 1)
    split = (col == 2 * (row % HALF) + row // HALF).astype(BF16)
    merge = (col == HALF * (row % 2) + row // 2).astype(BF16)
    eye = (row == col).astype(BF16)[:HALF, :HALF]

    for ref, width in ((y1w, 2), (y2w, 1), (g2w, 1), (x2w, 2), (x1w, 1), (b_w, 2), (b_x1, 2), (f_y2, 2), (c_w, 1)):
        rows = width * HALF
        zero = jnp.zeros((rows, CELLS), BF16)

        @pl.when(jnp.logical_not(has_lo))
        def _():
            ref[:rows] = zero

        @pl.when(jnp.logical_not(has_hi))
        def _():
            ref[rows + PAIR :] = zero

    pl.when(home_here)(kern_local.wait)
    pl.when(jnp.logical_not(home_here))(kern_remote.wait_recv)
    pl.when(jnp.logical_not(jnp.logical_or(home_here, relays)))(forward_start)

    def band(step, carry):
        which, b_off = step // 3, step % 3
        blank = jnp.zeros((HALF, HALF), BF16)
        for c_off in range(3):
            taps = [kern[which, 9 * depth + 3 * b_off + c_off] for depth in range(3)]
            line = jnp.concatenate(taps, 1)
            back = [kern[which, 26 - (9 * depth + 3 * b_off + c_off)] for depth in range(3)]
            line_t = lax.dot_general(
                eye, jnp.concatenate(back, 0), (((1,), (1,)), ((), ())), preferred_element_type=F32
            ).astype(BF16)
            for plane in range(2):
                where = (which, pl.ds(pl.multiple_of(b_off * PAIR, PAIR) + plane * HALF, HALF), pl.ds(c_off * 256, 256))
                order = (lambda t: [t, blank]) if plane == 0 else (lambda t: [blank, t])
                toep[where] = jnp.concatenate(order(line), 1)
                toep_t[where] = jnp.concatenate(order(line_t), 1)
        return carry

    def bands(first, last):
        lax.fori_loop(first, last, band, 0)

    pl.when(home_here)(lambda: bands(0, 6 * PAIRS))
    pl.when(jnp.logical_not(home_here))(lambda: bands(0, 2 * PAIRS))
    pl.when(home_here)(forward_start)

    def halo(index, ref, width):
        rows = width * HALF

        def copy(side, source, target, device):
            return pltpu.make_async_remote_copy(
                ref.at[pl.ds(source, rows)], ref.at[pl.ds(target, rows)],
                halo_send.at[index, side], halo_recv.at[index, side],
                device_id=device, device_id_type=MESH,
            )

        low = copy(0, rows, rows + PAIR, lo_dev)
        high = copy(1, PAIR, 0, hi_dev)
        return low, high

    def halo_start(*spec):
        low, high = halo(*spec)
        pl.when(has_lo)(low.start)
        pl.when(has_hi)(high.start)

    def halo_wait(*spec):
        low, high = halo(*spec)
        pl.when(has_lo)(high.wait_recv)
        pl.when(has_hi)(low.wait_recv)

    def halo_done(*spec):
        low, high = halo(*spec)
        pl.when(has_lo)(low.wait_send)
        pl.when(has_hi)(high.wait_send)

    def arrived(index):
        init_copy(index, state_ref, down_dev).wait_recv()
        return jnp.dot(split, raw[index].reshape(PAIR, CELLS), preferred_element_type=F32)

    def out_copy(index, out, half):
        local = pltpu.make_async_copy(stage.at[index], out.at[pl.ds(half * HALF, HALF)], out_send.at[index])
        remote = pltpu.make_async_remote_copy(
            stage.at[index], out.at[pl.ds(half * HALF, HALF)], out_send.at[index], out_recv.at[index],
            device_id=(section, slab), device_id_type=MESH,
        )
        return local, remote

    outs = ((out_fwd, 0), (out_fwd, 1), (out_back, 0), (out_back, 1), (out_grad, 0), (out_grad, 1))

    def out_start(index, value):
        rows = jnp.dot(merge, value, preferred_element_type=F32).astype(BF16)
        stage[index] = rows.reshape(HALF, 2, CELLS)
        local, remote = out_copy(index, *outs[index])
        pl.when(home_here)(local.start)
        pl.when(jnp.logical_not(home_here))(remote.start)

    edge_row = lax.broadcasted_iota(jnp.int32, (PAIR, CELLS), 0)
    outside = (
        jnp.logical_and(edge_row < HALF, jnp.logical_not(has_lo)),
        jnp.logical_and(edge_row >= HALF, jnp.logical_not(has_hi)),
    )

    def inside(side, value):
        return jnp.where(outside[side], 0.0, value).astype(BF16)

    halos = {
        "y1": (0, y1w, 2), "y2": (1, y2w, 1), "g2": (2, g2w, 1), "x2": (3, x2w, 2), "x1": (4, x1w, 1),
        "w": (5, b_w, 2), "bx1": (6, b_x1, 2), "fy2": (7, f_y2, 2), "cw": (8, c_w, 1),
    }

    y1w[PAIR : 2 * PAIR] = arrived(0).astype(BF16)
    halo_start(*halos["y1"])
    relay_on(1)
    pl.when(relays)(forward_start)
    pl.when(jnp.logical_not(home_here))(lambda: bands(2 * PAIRS, 4 * PAIRS))
    y2w[HALF : HALF + PAIR] = arrived(1).astype(BF16)
    halo_start(*halos["y2"])
    relay_on(3)
    init_start(2, grad_ref, head_grad_ref, *down)
    pl.when(jnp.logical_not(home_here))(lambda: bands(4 * PAIRS, 6 * PAIRS))
    g2w[HALF : HALF + PAIR] = arrived(3).astype(BF16)
    halo_start(*halos["g2"])
    x2w[PAIR : 2 * PAIR] = arrived(5).astype(BF16)
    halo_start(*halos["x2"])

    sides = [(side, pl.ds(side * PAIR, PAIR), pl.ds(side * PAIR, 4 * HALF)) for side in range(2)]

    def zeta_upper(pair, upper):
        for side, rows, wide in sides:
            zeta[rows] = conv_pair(upper[wide], toep[2 * pair + 1])

    def undo_second(lower, second):
        for side, rows, wide in sides:
            second[rows] = inside(side, lower[rows].astype(F32) - silu_slope(zeta[rows])[0])

    def undo_first(pair, upper, second):
        silu, slope = silu_slope(conv_pair(second[...], toep[2 * pair]))
        return (upper[PAIR : 2 * PAIR].astype(F32) - silu).astype(BF16), slope

    def grad_inner(lower_grad, inner):
        for side, rows, wide in sides:
            inner[rows] = inside(side, silu_slope(zeta[rows])[1] * lower_grad[rows].astype(F32))

    def forward(pair, upper, lower, mixed, ready=lambda: None):
        for side, rows, wide in sides:
            z = conv_pair(lower[wide], toep[2 * pair])
            mixed[rows] = inside(side, upper[rows].astype(F32) + silu_slope(z)[0])
        ready()
        z = conv_pair(mixed[...], toep[2 * pair + 1])
        return (lower[PAIR : 2 * PAIR].astype(F32) + silu_slope(z)[0]).astype(BF16)

    halo_wait(*halos["y1"])
    zeta_upper(1, y1w)
    x1w[HALF : HALF + PAIR] = arrived(4).astype(BF16)
    halo_start(*halos["x1"])
    halo_wait(*halos["y2"])
    undo_second(y2w, b_x2)
    first, slope = undo_first(1, y1w, b_x2)
    b_x1[PAIR : 2 * PAIR] = first
    halo_start(*halos["bx1"])
    relay_on(2)
    halo_wait(*halos["g2"])
    grad_inner(g2w, b_u)
    h1 = conv_pair(b_u[...], toep_t[3]) + arrived(2)
    b_w[PAIR : 2 * PAIR] = (slope * h1).astype(BF16)
    halo_start(*halos["w"])

    halo_wait(*halos["x2"])
    halo_wait(*halos["x1"])
    f_y2[PAIR : 2 * PAIR] = forward(0, x1w, x2w, f_y1)
    halo_start(*halos["fy2"])

    halo_wait(*halos["bx1"])
    zeta_upper(0, b_x1)
    undo_second(b_x2, c_x2)
    out_start(3, c_x2[HALF : HALF + PAIR])
    first, slope = undo_first(0, b_x1, c_x2)
    out_start(2, first)
    halo_wait(*halos["w"])
    for side, rows, wide in sides:
        h2[rows] = g2w[rows].astype(F32) + conv_pair(b_w[wide], toep_t[2])
    grad_inner(h2, c_u)
    h1 = h1 + conv_pair(c_u[...], toep_t[1])
    c_w[HALF : HALF + PAIR] = (slope * h1).astype(BF16)
    halo_start(*halos["cw"])
    out_start(4, h1.astype(BF16))

    halo_wait(*halos["fy2"])
    out_start(1, forward(1, f_y1, f_y2, d_y1, lambda: out_start(0, d_y1[HALF : HALF + PAIR])))

    halo_wait(*halos["cw"])
    out_start(5, (h2[HALF : HALF + PAIR] + conv_pair(c_w[...], toep_t[0])).astype(BF16))

    for index in range(6):
        init_done(index, *(down if index < 4 else up))
        if index in RELAYED:
            pl.when(relays)(relay_out(index).wait_send)
        local, remote = out_copy(index, *outs[index])
        pl.when(home_here)(local.wait)
        pl.when(jnp.logical_not(home_here))(remote.wait)
    pl.when(home_here)(kern_remote.wait_send)
    for spec in halos.values():
        halo_done(*spec)


def settle_kernel(in_0, in_1, in_2, out_0, out_1, out_2, sems):
    copies = [
        pltpu.make_async_copy(source, target, sems.at[i])
        for i, (source, target) in enumerate(((in_0, out_0), (in_1, out_1), (in_2, out_2)))
    ]
    for copy in copies:
        copy.start()
    for copy in copies:
        copy.wait()


def shards(fwd_states, back_states, back_grads, batch_in, head_state, head_grad, couplings):
    n_section, n_slab = lax.axis_size("section"), lax.axis_size("slab")
    anywhere = pl.BlockSpec(memory_space=pl.ANY)
    field = lambda planes: pltpu.VMEM((planes * HALF, CELLS), BF16)
    dma = pltpu.SemaphoreType.DMA
    out = jax.ShapeDtypeStruct((PAIR, 2, CELLS), BF16)
    fields = (fwd_states[0], back_states[0], back_grads[0], batch_in, head_state, head_grad, couplings[0])
    results = pl.pallas_call(
        functools.partial(step_kernel, n_section, n_slab),
        out_shape=(out, out, out),
        in_specs=[pl.BlockSpec(memory_space=pltpu.HBM)] * 7,
        out_specs=(anywhere,) * 3,
        scratch_shapes=[
            pltpu.VMEM((6, HALF, 2, CELLS), BF16),
            pltpu.VMEM((4, HALF, 2, CELLS), BF16),
            pltpu.VMEM(couplings.shape[1:], BF16),
            pltpu.VMEM((2 * PAIRS, 3 * PAIR, 12 * HALF), BF16),
            pltpu.VMEM((2 * PAIRS, 3 * PAIR, 12 * HALF), BF16),
            field(6), field(4), field(4), field(4), field(6),
            field(4), field(4), field(6), field(6),
            field(4), field(4), field(4),
            field(4), field(6), field(4),
            pltpu.VMEM((2 * PAIR, CELLS), F32),
            pltpu.VMEM((2 * PAIR, CELLS), F32),
            pltpu.VMEM((6, HALF, 2, CELLS), BF16),
            dma((6,)), dma((6,)), dma((4,)), dma((4,)), dma((9, 2)), dma((9, 2)), dma((6,)), dma((6,)), dma((3,)),
        ],
        compiler_params=pltpu.CompilerParams(collective_id=0, has_side_effects=True, vmem_limit_bytes=32 << 20),
    )(*(pltpu.with_memory_space_constraint(field, pltpu.HBM) for field in fields))

    settled = pl.pallas_call(
        settle_kernel,
        out_shape=(out, out, out),
        in_specs=[anywhere] * 3,
        out_specs=(pl.BlockSpec(memory_space=pltpu.HBM),) * 3,
        scratch_shapes=[dma((3,))],
        compiler_params=pltpu.CompilerParams(vmem_limit_bytes=4 << 20),
    )(*results)
    return tuple(value[None] for value in settled)


def solution(mesh):
    return jax.shard_map(
        shards,
        mesh=mesh,
        in_specs=(
            P("section", None, "slab", None),
            P("section", None, "slab", None),
            P("section", None, "slab", None),
            P(None, "slab", None),
            P(None, "slab", None),
            P(None, "slab", None),
            P("section", None, None, None, None),
        ),
        out_specs=(
            P("section", None, "slab", None),
            P("section", None, "slab", None),
            P("section", None, "slab", None),
        ),
        check_vma=False,
    )
```
